256 devices in a mesh: pair: 64 (over z, x, core), orb: 4 (over y).
Axes of the slice: x: 4, y: 4, z: 8, core: 2. Of those that a mesh axis runs over, the one named last changes fastest.
Arguments:
- integrals: bfloat16 [4096, 8, 128, 128], P('pair'), may hold values from -6 to 6
- screen: int32 [2, 4096, 8], P(None, 'pair'), may hold values from 0 to 95
- occupied: bfloat16 [12288, 32], P(('pair', 'orb')), may hold values from -0.3125 to 0.3125
- virtual: bfloat16 [12288, 512], P(('pair', 'orb')), may hold values from -0.5 to 0.5
- pair_index: int32 [2, 4096], replicated, may hold values from 0 to 12287
Outputs:
- mo_block: bfloat16 [4, 256, 512, 512], P('orb', 'pair')
The draws below stay inside these ranges and needn't reach their ends.
All inputs are finite; a program needn't handle non-finite values.
Results may differ from the reference program's by a relative error of at most 0.0064.
Values may be sent and summed in bfloat16 or wider, within the bound.
No kernel may reach another device: no remote copies, remote signals or barrier semaphores. Data moves between devices by JAX's collectives and lax.ppermute only.
A program may use at most 192 MiB of HBM per device.

```python
import jax
import jax.numpy as jnp
from jax import lax

BLK = 128
NBLK = 96
NOB = 32
NVB = 512
KB = 8
ROWS_DEV = 64
NBF = 12288
PAIRS = 4096
IO = 8
N_PAIR = 64
N_ORB = 4


def set_ends(array, stream_key, smallest, high):
    place = [jax.random.randint(jax.random.fold_in(stream_key, axis), (), 0, length) for axis, length in enumerate(array.shape)]
    main_axis = array.shape.index(max(array.shape))
    neighbour = place[:main_axis] + [(place[main_axis] + 1) % array.shape[main_axis]] + place[main_axis + 1:]
    return array.at[tuple(place)].set(smallest).at[tuple(neighbour)].set(high)


def shard_levels(stream_key, extent, split, smallest, top_value):
    gain = 1.0
    for axis_at, blocks in split:
        steps = jax.random.uniform(jax.random.fold_in(jax.random.fold_in(stream_key, 6), axis_at), (blocks,), jnp.float32, smallest / len(split), top_value / len(split))
        gain = gain * jnp.repeat(jnp.exp(steps), extent[axis_at] // blocks).reshape((-1,) + (1,) * (len(extent) - 1 - axis_at))
    return gain


def bell_draw(stream_key, shape, scale, most, cuts=(), kind=jnp.bfloat16):
    drawn = scale * jax.random.normal(stream_key, shape, jnp.float32)
    if cuts:
        drawn = drawn * shard_levels(stream_key, shape, cuts, -0.22, 0.18)
    return jnp.clip(drawn, -most, most).astype(kind)


def setup_inputs(seed: int = 0) -> dict:
    streams_of = jax.random.split(jax.random.key(seed), 6)
    integrals = bell_draw(streams_of[0], (PAIRS, KB, BLK, BLK), 1.0, 6.0, ((0, 64),))
    screen = set_ends(jax.random.randint(streams_of[1], (2, PAIRS, KB), 0, NBLK), jax.random.fold_in(streams_of[1], 1), 0, NBLK - 1).astype(jnp.int32)
    occupied = bell_draw(streams_of[2], (NBF, NOB), (BLK * 3) ** -0.5, 0.3125, ((0, 256),))
    virtual = bell_draw(streams_of[3], (NBF, NVB), (ROWS_DEV * N_PAIR // 32 + 1) ** -0.5, 0.5, ((0, 256),))
    pair_index = set_ends(jax.random.randint(streams_of[4], (2, PAIRS), 0, NBF), jax.random.fold_in(streams_of[4], 1), 0, NBF - 1).astype(jnp.int32)
    return dict(integrals=integrals, screen=screen, occupied=occupied, virtual=virtual, pair_index=pair_index)


def reference(integrals, screen, occupied, virtual, pair_index):
    blocks = occupied.reshape(NBLK, BLK, NOB)

    def first_half(items):
        values, mrows, nrows = items
        coef_m = blocks[mrows].astype(jnp.float32)
        coef_n = blocks[nrows].astype(jnp.float32)
        half_one = jnp.einsum("kmn,kmi->kni", values.astype(jnp.float32), coef_m).astype(jnp.bfloat16)
        return jnp.einsum("knj,kni->ij", coef_n, half_one.astype(jnp.float32)).astype(jnp.bfloat16)

    halves = lax.map(first_half, (integrals, screen[0], screen[1]))
    left = virtual[pair_index[0]]
    right = virtual[pair_index[1]]

    def second_half(occ_index):
        column = lax.dynamic_index_in_dim(halves, occ_index, 1, keepdims=False)
        weighted = (left[:, None, :].astype(jnp.float32) * column[:, :, None].astype(jnp.float32)).astype(jnp.bfloat16)
        flat = weighted.reshape(PAIRS, NOB * NVB)
        result = jnp.dot(flat.T, right, preferred_element_type=jnp.float32)
        return result.astype(jnp.bfloat16).reshape(NOB, NVB, NVB)

    per_first = lax.map(second_half, jnp.arange(NOB, dtype=jnp.int32))
    arranged = per_first.reshape(N_ORB, IO, NOB, NVB, NVB).transpose(0, 2, 1, 3, 4)
    return arranged.reshape(N_ORB, NOB * IO, NVB, NVB)
```

```python
import functools

import jax
import jax.numpy as jnp
from jax import lax
from jax.sharding import PartitionSpec as P
from jax.experimental import pallas as pl
from jax.experimental.pallas import tpu as pltpu

BLK = 128


def k2_body(npc, rows, nr, idx_ref, h_ref, *refs):
    pieces = refs[:npc]; out_ref = refs[npc]
    stage, V, L, LT, R, W, sem = refs[npc+1:]
    offs=[0]
    for n in rows: offs.append(offs[-1]+n)
    for i in range(npc):
        pltpu.make_async_copy(pieces[i], stage.at[pl.ds(offs[i],rows[i])], sem.at[i]).start()
    for i in range(npc):
        pltpu.make_async_copy(pieces[i], stage.at[pl.ds(offs[i],rows[i])], sem.at[i]).wait()
        step=64
        while rows[i]%step: step//=2
        def conv(t,_,base=offs[i],step=step):
            r0=pl.multiple_of(base+t*step,16)
            for c in range(4):
                x=stage[pl.ds(r0,step),c*128:(c+1)*128].astype(jnp.float32)
                V[pl.ds(r0*4+c,step,stride=4),:]=x
            return 0
        lax.fori_loop(0,rows[i]//step,conv,0)
    CH=128
    def chunk(ci,_):
        p0=pl.multiple_of(ci*CH,CH)
        for side in range(2):
            def g(t,_):
                for u in range(16):
                    i=t*16+u
                    r=idx_ref[side,p0+i]
                    L[pl.ds(pl.multiple_of(side*CH*4+i*4,4),4),:]=V[pl.ds(pl.multiple_of(r*4,4),4),:]
                return 0
            lax.fori_loop(0,CH//16,g,0)
        for c in range(4):
            a=L[pl.ds(c,CH,stride=4),:]
            LT[c*128:(c+1)*128,pl.ds(p0,CH)]=a.T.astype(jnp.bfloat16)
            b=L[pl.ds(CH*4+c,CH,stride=4),:]
            R[pl.ds(p0,CH),c*128:(c+1)*128]=b.astype(jnp.bfloat16)
        return 0
    lax.fori_loop(0,nr//CH,chunk,0)
    AB=256
    def mm(t,_):
        jk=t//2; a0=pl.multiple_of((t%2)*AB,AB)
        h=h_ref[pl.ds(jk,1),:].astype(jnp.bfloat16)
        W[...]=LT[pl.ds(a0,AB),:]*h
        out_ref[jk,pl.ds(a0,AB),:]=jnp.dot(W[...],R[...],preferred_element_type=jnp.float32).astype(jnp.bfloat16)
        return 0
    lax.fori_loop(0,8,mm,0)
def k2(idx,h,pieces):
    rows=[p.shape[0] for p in pieces]; n=len(pieces); tot=sum(rows); nr=idx.shape[1]
    return pl.pallas_call(functools.partial(k2_body,n,rows,nr),
        out_shape=jax.ShapeDtypeStruct((4,512,512),jnp.bfloat16),
        in_specs=[pl.BlockSpec(memory_space=pltpu.SMEM),pl.BlockSpec(memory_space=pltpu.VMEM)]+[pl.BlockSpec(memory_space=pl.ANY)]*n,
        out_specs=pl.BlockSpec(memory_space=pltpu.VMEM),
        scratch_shapes=[pltpu.VMEM((tot,512),jnp.bfloat16),pltpu.VMEM((tot*4,128),jnp.float32),
            pltpu.VMEM((128*8,128),jnp.float32),pltpu.VMEM((512,nr),jnp.bfloat16),pltpu.VMEM((nr,512),jnp.bfloat16),
            pltpu.VMEM((256,nr),jnp.bfloat16),pltpu.SemaphoreType.DMA((n,))],
        compiler_params=pltpu.CompilerParams(vmem_limit_bytes=60*1024*1024),
        name="gather_scale_dot")(idx,h,*pieces)


def body(integrals, screen, occupied, virtual, pair_index):
    occ_all, vir_all = (
        lax.all_gather(occupied, ("pair", "orb"), axis=0, tiled=True),
        lax.all_gather(virtual, ("pair", "orb"), axis=0, tiled=True),
    )
    orb_count = lax.axis_size("orb")
    first_count = occ_all.shape[1] // orb_count
    own_cols = lax.dynamic_slice_in_dim(
        occ_all, lax.axis_index("orb") * first_count, first_count, 1
    )
    block_count = occ_all.shape[0] // BLK
    blocks_all = occ_all.reshape(block_count, BLK, occ_all.shape[1])
    blocks_own = own_cols.reshape(block_count, BLK, first_count)
    coef_m = blocks_own[screen[0]]
    coef_n = blocks_all[screen[1]]
    half_one = jnp.einsum(
        "pkmn,pkmi->pkni", integrals, coef_m, preferred_element_type=jnp.float32
    ).astype(jnp.bfloat16)
    half = jnp.einsum(
        "pknj,pkni->pji", coef_n, half_one, preferred_element_type=jnp.float32
    ).astype(jnp.bfloat16)
    local_rows = half.reshape(half.shape[0], half.shape[1] * first_count)
    owned = lax.all_to_all(local_rows, "pair", split_axis=1, concat_axis=0, tiled=True)
    out = k2(pair_index, owned.T.astype(jnp.float32), [vir_all])
    return out[None]


def solution(mesh):
    placed = (
        P("pair", None, None, None),
        P(None, "pair", None),
        P(("pair", "orb"), None),
        P(("pair", "orb"), None),
        P(),
    )
    return jax.shard_map(
        body, mesh=mesh, in_specs=placed, out_specs=P("orb", "pair", None, None), check_vma=False
    )
```

```python
import functools

import jax
import jax.numpy as jnp
from jax import lax
from jax.experimental import pallas as pl
from jax.experimental.pallas import tpu as pltpu
from jax.sharding import PartitionSpec as P

BLK = 128
NZ, NX, NY = 8, 4, 4
BF, F32 = jnp.bfloat16, jnp.float32


def pair_moves(dz=0, dx=0, dc=0):
    moves = []
    for z in range(NZ):
        for x in range(NX):
            for c in range(2):
                src = (((z + dz) % NZ) * NX + (x + dx) % NX) * 2 + (c + dc) % 2
                moves.append((src, (z * NX + x) * 2 + c))
    return moves


def fetch(value, axis, step):
    if axis == "y":
        return lax.ppermute(value, "orb", [((y + step) % NY, y) for y in range(NY)])
    return lax.ppermute(value, "pair", pair_moves(**{"d" + axis: step}))


def rows(*parts):
    return jnp.concatenate(parts, axis=0)


def four(value, axis):
    return [value] + [fetch(value, axis, step) for step in (1, 2, 3)]


def cross(value, step, swap):
    moves = []
    for z in range(NZ):
        for x in range(NX):
            for c in range(2):
                for y in range(NY):
                    ex, ey = (x, (y + step) % NY) if c == swap else ((x + step) % NX, y)
                    src = ((z * NX + ex) * 2 + c) * NY + ey
                    moves.append((src, ((z * NX + x) * 2 + c) * NY + y))
    return lax.ppermute(value, ("pair", "orb"), moves)


def ring(value, move):
    half = value.shape[0] // 2
    up, down = move(value, 1), move(value, -1)
    far = [move(up[:half], 1), move(down[half:], -1)]
    return [value, up, *far, down]


def gather_virtual(v):
    near = rows(fetch(v, "z", -1), v, fetch(v, "z", 1))
    far_up = fetch(near, "z", 3)
    far_down = fetch(near[48:], "z", -3)
    z_all = rows(near, far_up, far_down)
    b = rows(*ring(z_all, lambda t, d: cross(t, d, 0)))
    arrays = ring(b, lambda t, d: cross(t, d, 1))
    arrays = arrays + [fetch(t, "c", 1) for t in arrays]
    copies, at = [], 0
    for k, t in enumerate(arrays):
        copies.append((k, 0, at, t.shape[0]))
        at += t.shape[0]
    return arrays, copies


def place():
    pair, y = lax.axis_index("pair"), lax.axis_index("orb")
    return pair // 8, (pair // 2) % NX, pair % 2, y


def virtual_place(index):
    mz, mx, mc, my = place()
    device, local = index // 48, index % 48
    pair = device // NY
    dy = (device - my) % NY
    dc = (pair - mc) % 2
    dx = (pair // 2 - mx) % NX
    dz = (pair // 8 - mz) % NZ
    inner, outer = jnp.where(pair % 2 == 0, dy, dx), jnp.where(pair % 2 == 0, dx, dy)
    return dc * 6144 + outer * 1536 + inner * 384 + (dz + 1) % NZ * 48 + local


def gather_occupied(o):
    _, _, mc, my = place()
    ot = o.T
    row = jnp.zeros((32, 192), BF)
    for step, piece in enumerate(four(ot, "y")):
        row = lax.dynamic_update_slice(row, piece, (0, ((my + step) % NY) * 48))
    other = fetch(row, "c", 1)
    chip = jnp.where(mc == 0, jnp.concatenate([row, other], 1), jnp.concatenate([other, row], 1))
    mine = lax.dynamic_slice_in_dim(chip, mc * 16, 16, 0)
    cols = lambda *t: jnp.concatenate(t, axis=1)
    near = cols(fetch(mine, "z", -1), mine, fetch(mine, "z", 1))
    z_all = cols(near, fetch(near, "z", 3), fetch(near[:, 384:], "z", -3))
    mine = cols(*four(z_all, "x"))
    other = fetch(mine, "c", 1)
    return jnp.where(mc == 0, rows(mine, other), rows(other, mine))


def block_place(block):
    mz, mx, _, _ = place()
    chip = block // 3
    dx = (chip - mx) % NX
    dz = (chip // NX - mz) % NZ
    return (dx * 8 + (dz + 1) % NZ) * 3 + block % 3


def half_kernel(count, scr_ref, ints_ref, own_ref, occ_ref, out_ref):
    step = pl.program_id(0)
    firsts, coefs = [], []
    for t in range(count):
        p = step * count + t
        for s in range(8):
            m = pl.multiple_of(scr_ref[0, p, s] * BLK, BLK)
            first = jnp.dot(own_ref[:, pl.ds(m, BLK)], ints_ref[t, s], preferred_element_type=F32)
            firsts.append(first.astype(BF))
    for t in range(count):
        p = step * count + t
        coefs = []
        for s in range(8):
            n = pl.multiple_of(scr_ref[1, p, s] * BLK, BLK)
            coefs.append(occ_ref[:, pl.ds(n, BLK)])
        out_ref[t] = lax.dot_general(
            jnp.concatenate(coefs, axis=1), jnp.concatenate(firsts[8 * t : 8 * t + 8], axis=1),
            (((1,), (1,)), ((), ())), preferred_element_type=F32,
        ).astype(out_ref.dtype)


def half_transform(integrals, blocks, own, occ):
    pairs, count = integrals.shape[0], 8
    return pl.pallas_call(
        functools.partial(half_kernel, count),
        grid_spec=pltpu.PrefetchScalarGridSpec(
            num_scalar_prefetch=1,
            grid=(pairs // count,),
            in_specs=[
                pl.BlockSpec((count, 8, BLK, BLK), lambda i, s: (i, 0, 0, 0)),
                pl.BlockSpec(own.shape, lambda i, s: (0, 0)),
                pl.BlockSpec(occ.shape, lambda i, s: (0, 0)),
            ],
            out_specs=pl.BlockSpec((count, 32, own.shape[0]), lambda i, s: (i, 0, 0)),
        ),
        out_shape=jax.ShapeDtypeStruct((pairs, 32, own.shape[0]), BF),
        compiler_params=pltpu.CompilerParams(vmem_limit_bytes=56 * 1024 * 1024),
        cost_estimate=pl.CostEstimate(flops=3 * 10**8, bytes_accessed=18 * 10**6, transcendentals=0),
        name="half_transform",
    )(blocks, integrals, own, occ)


def last_kernel(copies, arrays, idx_ref, h_ref, *refs):
    pieces, out_ref = refs[:arrays], refs[arrays]
    stage, table, picked, left, right, scaled, sem = refs[arrays + 1 :]
    total, pairs = stage.shape[0], idx_ref.shape[0] // 2
    order = sorted(copies, key=lambda c: c[2])
    dma = [
        pltpu.make_async_copy(pieces[k].at[pl.ds(src, n)], stage.at[pl.ds(dst, n)], sem.at[j])
        for j, (k, src, dst, n) in enumerate(order)
    ]
    for copy in dma:
        copy.start()
    done = 0
    for part in range(6):
        end = (part + 1) * (total // 6)
        while done < len(dma) and order[done][2] < end:
            dma[done].wait()
            done += 1

        def widen(t, _, base=part * (total // 6)):
            r0 = pl.multiple_of(base + t * 64, 64)
            for c in range(4):
                block = stage[pl.ds(r0, 64), c * 128 : (c + 1) * 128].astype(F32)
                table[pl.ds(r0 * 4 + c, 64, stride=4), :] = block
            return 0

        lax.fori_loop(0, total // 6 // 64, widen, 0)
    CH = 128

    def chunk(ci, _):
        p0 = pl.multiple_of(ci * CH, CH)
        for side in range(2):

            def pick(t, _):
                base = side * pairs + p0 + t * 32
                got = [table[pl.ds(pl.multiple_of(idx_ref[base + u], 4), 4), :] for u in range(32)]
                to = pl.multiple_of((side * CH + t * 32) * 4, 128)
                for u in range(32):
                    picked[pl.ds(to + 4 * u, 4), :] = got[u]
                return 0

            lax.fori_loop(0, CH // 32, pick, 0)
        for c in range(4):
            block = picked[pl.ds(c, CH, stride=4), :]
            left[c * 128 : (c + 1) * 128, pl.ds(p0, CH)] = block.T.astype(BF)
            block = picked[pl.ds(CH * 4 + c, CH, stride=4), :]
            right[pl.ds(p0, CH), c * 128 : (c + 1) * 128] = block.astype(BF)
        return 0

    lax.fori_loop(0, pairs // CH, chunk, 0)

    def multiply(t, _):
        jk, a0 = t // 2, pl.multiple_of((t % 2) * 256, 256)
        h = h_ref[pl.ds(jk, 1), :].astype(BF)
        scaled[...] = left[pl.ds(a0, 256), :] * h
        out_ref[jk, pl.ds(a0, 256), :] = jnp.dot(scaled[...], right[...], preferred_element_type=F32).astype(BF)
        return 0

    lax.fori_loop(0, 8, multiply, 0)


def last_stage(index, h, arrays, copies):
    pairs, total = index.shape[0] // 2, sum(c[3] for c in copies)
    return pl.pallas_call(
        functools.partial(last_kernel, copies, len(arrays)),
        out_shape=jax.ShapeDtypeStruct((4, 512, 512), BF),
        in_specs=[pl.BlockSpec(memory_space=pltpu.SMEM), pl.BlockSpec(memory_space=pltpu.VMEM)]
        + [pl.BlockSpec(memory_space=pl.ANY)] * len(arrays),
        out_specs=pl.BlockSpec(memory_space=pltpu.VMEM),
        scratch_shapes=[
            pltpu.VMEM((total, 512), BF),
            pltpu.VMEM((total * 4, 128), F32),
            pltpu.VMEM((128 * 8, 128), F32),
            pltpu.VMEM((512, pairs), BF),
            pltpu.VMEM((pairs, 512), BF),
            pltpu.VMEM((256, pairs), BF),
            pltpu.SemaphoreType.DMA((len(copies),)),
        ],
        compiler_params=pltpu.CompilerParams(vmem_limit_bytes=60 * 1024 * 1024),
        cost_estimate=pl.CostEstimate(flops=9 * 10**9, bytes_accessed=15 * 10**6, transcendentals=0),
        name="gather_scale_dot",
    )(index, h, *arrays)


def stages(integrals, screen, occupied, virtual, pair_index):
    arrays, copies = gather_virtual(virtual)
    occ = gather_occupied(occupied)
    own = lax.dynamic_slice_in_dim(occ, lax.axis_index("orb") * 8, 8, 0)
    half = half_transform(integrals, block_place(screen), own, occ)
    sent = half.transpose(1, 2, 0).reshape(64, 4, half.shape[0])
    owned = lax.all_to_all(sent, "pair", 0, 0)
    h = owned.transpose(1, 0, 2).reshape(4, -1).astype(F32)
    return last_stage(virtual_place(pair_index).reshape(-1) * 4, h, arrays, copies)[None]


def solution(mesh):
    placed = (
        P("pair", None, None, None),
        P(None, "pair", None),
        P(("pair", "orb"), None),
        P(("pair", "orb"), None),
        P(),
    )
    return jax.shard_map(stages, mesh=mesh, in_specs=placed, out_specs=P("orb", "pair", None, None), check_vma=False)
```

```python
import functools

import jax
import jax.numpy as jnp
from jax import lax
from jax.experimental import pallas as pl
from jax.experimental.pallas import tpu as pltpu
from jax.sharding import PartitionSpec as P

BLK = 128
NZ, NX, NY = 8, 4, 4
BF, F32 = jnp.bfloat16, jnp.float32


def pair_moves(dz=0, dx=0, dc=0):
    moves = []
    for z in range(NZ):
        for x in range(NX):
            for c in range(2):
                src = (((z + dz) % NZ) * NX + (x + dx) % NX) * 2 + (c + dc) % 2
                moves.append((src, (z * NX + x) * 2 + c))
    return moves


def fetch(value, axis, step):
    if axis == "y":
        return lax.ppermute(value, "orb", [((y + step) % NY, y) for y in range(NY)])
    return lax.ppermute(value, "pair", pair_moves(**{"d" + axis: step}))


def rows(*parts):
    return jnp.concatenate(parts, axis=0)


def four(value, axis):
    return [value] + [fetch(value, axis, step) for step in (1, 2, 3)]


def cross(value, step, swap):
    moves = []
    for z in range(NZ):
        for x in range(NX):
            for c in range(2):
                for y in range(NY):
                    ex, ey = (x, (y + step) % NY) if c == swap else ((x + step) % NX, y)
                    src = ((z * NX + ex) * 2 + c) * NY + ey
                    moves.append((src, ((z * NX + x) * 2 + c) * NY + y))
    return lax.ppermute(value, ("pair", "orb"), moves)


def ring(value, move):
    half = value.shape[0] // 2
    up, down = move(value, 1), move(value, -1)
    far = [move(up[:half], 1), move(down[half:], -1)]
    return [value, up, *far, down]


def gather_virtual(v):
    near = rows(fetch(v, "z", -1), v, fetch(v, "z", 1))
    far_up = fetch(near, "z", 3)
    far_down = fetch(near[48:], "z", -3)
    z_all = rows(near, far_up, far_down)
    b = rows(*ring(z_all, lambda t, d: cross(t, d, 0)))
    arrays = ring(b, lambda t, d: cross(t, d, 1))
    arrays = arrays + [fetch(t, "c", 1) for t in arrays]
    copies, at = [], 0
    for k, t in enumerate(arrays):
        copies.append((k, 0, at, t.shape[0]))
        at += t.shape[0]
    return arrays, copies


def place():
    pair, y = lax.axis_index("pair"), lax.axis_index("orb")
    return pair // 8, (pair // 2) % NX, pair % 2, y


def virtual_place(index):
    mz, mx, mc, my = place()
    device, local = index // 48, index % 48
    pair = device // NY
    dy = (device - my) % NY
    dc = (pair - mc) % 2
    dx = (pair // 2 - mx) % NX
    dz = (pair // 8 - mz) % NZ
    inner, outer = jnp.where(pair % 2 == 0, dy, dx), jnp.where(pair % 2 == 0, dx, dy)
    return dc * 6144 + outer * 1536 + inner * 384 + (dz + 1) % NZ * 48 + local


def gather_occupied(o):
    _, _, mc, my = place()
    ot = o.T
    row = jnp.zeros((32, 192), BF)
    for step, piece in enumerate(four(ot, "y")):
        row = lax.dynamic_update_slice(row, piece, (0, ((my + step) % NY) * 48))
    other = fetch(row, "c", 1)
    chip = jnp.where(mc == 0, jnp.concatenate([row, other], 1), jnp.concatenate([other, row], 1))
    mine = lax.dynamic_slice_in_dim(chip, mc * 16, 16, 0)
    cols = lambda *t: jnp.concatenate(t, axis=1)
    near = cols(fetch(mine, "z", -1), mine, fetch(mine, "z", 1))
    z_all = cols(near, fetch(near, "z", 3), fetch(near[:, 384:], "z", -3))
    mine = cols(*four(z_all, "x"))
    other = fetch(mine, "c", 1)
    return jnp.where(mc == 0, rows(mine, other), rows(other, mine))


def block_place(block):
    mz, mx, _, _ = place()
    chip = block // 3
    dx = (chip - mx) % NX
    dz = (chip // NX - mz) % NZ
    return (dx * 8 + (dz + 1) % NZ) * 3 + block % 3


def half_kernel(group, scr_ref, own_ref, occ_ref, ints_ref, out_ref, ints, halves, sem):
    pairs = ints.shape[0]
    groups = pairs // group

    def copy(g):
        part = pl.ds(g * group, group)
        return pltpu.make_async_copy(ints_ref.at[part], ints.at[part], sem.at[g])

    for g in range(groups):
        copy(g).start()

    def step(g, _):
        copy(g).wait()
        firsts = []
        for t in range(group):
            p = g * group + t
            for s in range(8):
                m = pl.multiple_of(scr_ref[0, p, s] * BLK, BLK)
                first = jnp.dot(own_ref[:, pl.ds(m, BLK)], ints[p, s], preferred_element_type=F32)
                firsts.append(first.astype(BF))
        for t in range(group):
            p = g * group + t
            coefs = []
            for s in range(8):
                n = pl.multiple_of(scr_ref[1, p, s] * BLK, BLK)
                coefs.append(occ_ref[:, pl.ds(n, BLK)])
            value = lax.dot_general(
                jnp.concatenate(firsts[8 * t : 8 * t + 8], axis=1), jnp.concatenate(coefs, axis=1),
                (((1,), (1,)), ((), ())), preferred_element_type=F32,
            )
            halves[pl.ds(p, 8, stride=pairs), 0:32] = value
        return 0

    lax.fori_loop(0, groups, step, 0)
    for i in range(8):
        block = halves[i * pairs : (i + 1) * pairs, :].T
        out_ref[pl.ds(i, 32, stride=8), :] = block[0:32, :]


def half_transform(integrals, blocks, own, occ):
    pairs, group = integrals.shape[0], 8
    vmem = pl.BlockSpec(memory_space=pltpu.VMEM)
    return pl.pallas_call(
        functools.partial(half_kernel, group),
        in_specs=[pl.BlockSpec(memory_space=pltpu.SMEM), vmem, vmem, pl.BlockSpec(memory_space=pl.ANY)],
        out_specs=vmem,
        out_shape=jax.ShapeDtypeStruct((256, pairs), F32),
        scratch_shapes=[
            pltpu.VMEM(integrals.shape, BF),
            pltpu.VMEM((8 * pairs, 128), F32),
            pltpu.SemaphoreType.DMA((pairs // group,)),
        ],
        compiler_params=pltpu.CompilerParams(vmem_limit_bytes=48 * 1024 * 1024),
        cost_estimate=pl.CostEstimate(flops=3 * 10**8, bytes_accessed=18 * 10**6, transcendentals=0),
        name="half_transform",
    )(blocks, own, occ, integrals)


def last_kernel(copies, arrays, idx_ref, h_ref, *refs):
    pieces, out_ref = refs[:arrays], refs[arrays]
    stage, table, picked, left, right, scaled, sem = refs[arrays + 1 :]
    total, pairs = stage.shape[0], idx_ref.shape[0] // 2
    order = sorted(copies, key=lambda c: c[2])
    dma = [
        pltpu.make_async_copy(pieces[k].at[pl.ds(src, n)], stage.at[pl.ds(dst, n)], sem.at[j])
        for j, (k, src, dst, n) in enumerate(order)
    ]
    for copy in dma:
        copy.start()
    done = 0
    for part in range(6):
        end = (part + 1) * (total // 6)
        while done < len(dma) and order[done][2] < end:
            dma[done].wait()
            done += 1

        def widen(t, _, base=part * (total // 6)):
            r0 = pl.multiple_of(base + t * 64, 64)
            for c in range(4):
                block = stage[pl.ds(r0, 64), c * 128 : (c + 1) * 128].astype(F32)
                table[pl.ds(r0 * 4 + c, 64, stride=4), :] = block
            return 0

        lax.fori_loop(0, total // 6 // 64, widen, 0)
    CH = 128

    def chunk(ci, _):
        p0 = pl.multiple_of(ci * CH, CH)
        for side in range(2):

            def pick(t, _):
                base = side * pairs + p0 + t * 32
                got = [table[pl.ds(pl.multiple_of(idx_ref[base + u], 4), 4), :] for u in range(32)]
                to = pl.multiple_of((side * CH + t * 32) * 4, 128)
                for u in range(32):
                    picked[pl.ds(to + 4 * u, 4), :] = got[u]
                return 0

            lax.fori_loop(0, CH // 32, pick, 0)
        for c in range(4):
            block = picked[pl.ds(c, CH, stride=4), :]
            left[c * 128 : (c + 1) * 128, pl.ds(p0, CH)] = block.T.astype(BF)
            block = picked[pl.ds(CH * 4 + c, CH, stride=4), :]
            right[pl.ds(p0, CH), c * 128 : (c + 1) * 128] = block.astype(BF)
        return 0

    lax.fori_loop(0, pairs // CH, chunk, 0)

    def multiply(t, _):
        jk, a0 = t // 2, pl.multiple_of((t % 2) * 256, 256)
        h = h_ref[pl.ds(jk, 1), :].astype(BF)
        scaled[...] = left[pl.ds(a0, 256), :] * h
        out_ref[jk, pl.ds(a0, 256), :] = jnp.dot(scaled[...], right[...], preferred_element_type=F32).astype(BF)
        return 0

    lax.fori_loop(0, 8, multiply, 0)


def last_stage(index, h, arrays, copies):
    pairs, total = index.shape[0] // 2, sum(c[3] for c in copies)
    return pl.pallas_call(
        functools.partial(last_kernel, copies, len(arrays)),
        out_shape=jax.ShapeDtypeStruct((4, 512, 512), BF),
        in_specs=[pl.BlockSpec(memory_space=pltpu.SMEM), pl.BlockSpec(memory_space=pltpu.VMEM)]
        + [pl.BlockSpec(memory_space=pl.ANY)] * len(arrays),
        out_specs=pl.BlockSpec(memory_space=pltpu.VMEM),
        scratch_shapes=[
            pltpu.VMEM((total, 512), BF),
            pltpu.VMEM((total * 4, 128), F32),
            pltpu.VMEM((128 * 8, 128), F32),
            pltpu.VMEM((512, pairs), BF),
            pltpu.VMEM((pairs, 512), BF),
            pltpu.VMEM((256, pairs), BF),
            pltpu.SemaphoreType.DMA((len(copies),)),
        ],
        compiler_params=pltpu.CompilerParams(vmem_limit_bytes=60 * 1024 * 1024),
        cost_estimate=pl.CostEstimate(flops=9 * 10**9, bytes_accessed=15 * 10**6, transcendentals=0),
        name="gather_scale_dot",
    )(index, h, *arrays)


def stages(integrals, screen, occupied, virtual, pair_index):
    arrays, copies = gather_virtual(virtual)
    occ = gather_occupied(occupied)
    own = lax.dynamic_slice_in_dim(occ, lax.axis_index("orb") * 8, 8, 0)
    half = half_transform(integrals, block_place(screen), own, occ)
    sent = half.astype(BF).reshape(64, 4, half.shape[1])
    owned = lax.all_to_all(sent, "pair", 0, 0)
    h = owned.transpose(1, 0, 2).reshape(4, -1).astype(F32)
    return last_stage(virtual_place(pair_index).reshape(-1) * 4, h, arrays, copies)[None]


def solution(mesh):
    placed = (
        P("pair", None, None, None),
        P(None, "pair", None),
        P(("pair", "orb"), None),
        P(("pair", "orb"), None),
        P(),
    )
    return jax.shard_map(stages, mesh=mesh, in_specs=placed, out_specs=P("orb", "pair", None, None), check_vma=False)
```

```python
import functools

import jax
import jax.numpy as jnp
from jax import lax
from jax.experimental import pallas as pl
from jax.experimental.pallas import tpu as pltpu
from jax.sharding import PartitionSpec as P

BLK = 128
NZ, NX, NY = 8, 4, 4
BF, F32 = jnp.bfloat16, jnp.float32


def pair_moves(dz=0, dx=0, dc=0):
    moves = []
    for z in range(NZ):
        for x in range(NX):
            for c in range(2):
                src = (((z + dz) % NZ) * NX + (x + dx) % NX) * 2 + (c + dc) % 2
                moves.append((src, (z * NX + x) * 2 + c))
    return moves


def fetch(value, axis, step):
    if axis == "y":
        return lax.ppermute(value, "orb", [((y + step) % NY, y) for y in range(NY)])
    return lax.ppermute(value, "pair", pair_moves(**{"d" + axis: step}))


def rows(*parts):
    return jnp.concatenate(parts, axis=0)


def four(value, axis):
    return [value] + [fetch(value, axis, step) for step in (1, 2, 3)]


def cross(value, step, swap):
    moves = []
    for z in range(NZ):
        for x in range(NX):
            for c in range(2):
                for y in range(NY):
                    ex, ey = (x, (y + step) % NY) if c == swap else ((x + step) % NX, y)
                    src = ((z * NX + ex) * 2 + c) * NY + ey
                    moves.append((src, ((z * NX + x) * 2 + c) * NY + y))
    return lax.ppermute(value, ("pair", "orb"), moves)


def ring(value, move):
    half = value.shape[0] // 2
    up, down = move(value, 1), move(value, -1)
    far = [move(up[:half], 1), move(down[half:], -1)]
    return [value, up, *far, down]


def gather_virtual(v):
    near = rows(fetch(v, "z", -1), v, fetch(v, "z", 1))
    far_up = fetch(near, "z", 3)
    far_down = fetch(near[48:], "z", -3)
    z_all = rows(near, far_up, far_down)
    b = rows(*ring(z_all, lambda t, d: cross(t, d, 0)))
    arrays = ring(b, lambda t, d: cross(t, d, 1))
    arrays = arrays + [fetch(t, "c", 1) for t in arrays]
    copies, at = [], 0
    for k, t in enumerate(arrays):
        copies.append((k, 0, at, t.shape[0]))
        at += t.shape[0]
    return arrays, copies


def place():
    pair, y = lax.axis_index("pair"), lax.axis_index("orb")
    return pair // 8, (pair // 2) % NX, pair % 2, y


def virtual_place(index):
    mz, mx, mc, my = place()
    device, local = index // 48, index % 48
    pair = device // NY
    dy = (device - my) % NY
    dc = (pair - mc) % 2
    dx = (pair // 2 - mx) % NX
    dz = (pair // 8 - mz) % NZ
    inner, outer = jnp.where(pair % 2 == 0, dy, dx), jnp.where(pair % 2 == 0, dx, dy)
    return dc * 6144 + outer * 1536 + inner * 384 + (dz + 1) % NZ * 48 + local


def gather_occupied(o):
    _, _, mc, my = place()
    ot = o.T
    row = jnp.zeros((32, 192), BF)
    for step, piece in enumerate(four(ot, "y")):
        row = lax.dynamic_update_slice(row, piece, (0, ((my + step) % NY) * 48))
    other = fetch(row, "c", 1)
    chip = jnp.where(mc == 0, jnp.concatenate([row, other], 1), jnp.concatenate([other, row], 1))
    mine = lax.dynamic_slice_in_dim(chip, mc * 16, 16, 0)
    cols = lambda *t: jnp.concatenate(t, axis=1)
    near = cols(fetch(mine, "z", -1), mine, fetch(mine, "z", 1))
    z_all = cols(near, fetch(near, "z", 3), fetch(near[:, 384:], "z", -3))
    mine = cols(*four(z_all, "x"))
    other = fetch(mine, "c", 1)
    return jnp.where(mc == 0, rows(mine, other), rows(other, mine))


def block_place(block):
    mz, mx, _, _ = place()
    chip = block // 3
    dx = (chip - mx) % NX
    dz = (chip // NX - mz) % NZ
    return (dx * 8 + (dz + 1) % NZ) * 3 + block % 3


def half_kernel(group, scr_ref, own_ref, occ_ref, ints_ref, out_ref, ints, halves, sem):
    pairs = ints.shape[0]
    groups = pairs // group

    def copy(g):
        part = pl.ds(g * group, group)
        return pltpu.make_async_copy(ints_ref.at[part], ints.at[part], sem.at[g])

    for g in range(groups):
        copy(g).start()

    def step(g, _):
        copy(g).wait()
        firsts = []
        for t in range(group):
            p = g * group + t
            for s in range(8):
                m = pl.multiple_of(scr_ref[0, p, s] * BLK, BLK)
                first = jnp.dot(own_ref[:, pl.ds(m, BLK)], ints[p, s], preferred_element_type=F32)
                firsts.append(first.astype(BF))
        for t in range(group):
            p = g * group + t
            coefs = []
            for s in range(8):
                n = pl.multiple_of(scr_ref[1, p, s] * BLK, BLK)
                coefs.append(occ_ref[:, pl.ds(n, BLK)])
            value = lax.dot_general(
                jnp.concatenate(firsts[8 * t : 8 * t + 8], axis=1), jnp.concatenate(coefs, axis=1),
                (((1,), (1,)), ((), ())), preferred_element_type=F32,
            )
            halves[pl.ds(p, 8, stride=pairs), 0:32] = value
        return 0

    lax.fori_loop(0, groups, step, 0)
    for i in range(8):
        block = halves[i * pairs : (i + 1) * pairs, :].T
        out_ref[pl.ds(i, 32, stride=8), :] = block[0:32, :]


def half_transform(integrals, blocks, own, occ):
    pairs, group = integrals.shape[0], 8
    vmem = pl.BlockSpec(memory_space=pltpu.VMEM)
    return pl.pallas_call(
        functools.partial(half_kernel, group),
        in_specs=[pl.BlockSpec(memory_space=pltpu.SMEM), vmem, vmem, pl.BlockSpec(memory_space=pl.ANY)],
        out_specs=vmem,
        out_shape=jax.ShapeDtypeStruct((256, pairs), F32),
        scratch_shapes=[
            pltpu.VMEM(integrals.shape, BF),
            pltpu.VMEM((8 * pairs, 128), F32),
            pltpu.SemaphoreType.DMA((pairs // group,)),
        ],
        compiler_params=pltpu.CompilerParams(vmem_limit_bytes=48 * 1024 * 1024),
        cost_estimate=pl.CostEstimate(flops=3 * 10**8, bytes_accessed=18 * 10**6, transcendentals=0),
        name="half_transform",
    )(blocks, own, occ, integrals)


def last_kernel(copies, arrays, idx_ref, h_ref, *refs):
    pieces, out_ref = refs[:arrays], refs[arrays]
    stage, table, picked, left, right, scaled, rows_at, sem, isem = refs[arrays + 1 :]
    total = stage.shape[0]
    order = sorted(copies, key=lambda c: c[2])
    dma = [
        pltpu.make_async_copy(pieces[k].at[pl.ds(src, n)], stage.at[pl.ds(dst, n)], sem.at[j])
        for j, (k, src, dst, n) in enumerate(order)
    ]
    for slot in range(2):
        part = pl.ds(slot * 1024, 1024)
        pltpu.make_async_copy(idx_ref.at[part], rows_at.at[part], isem.at[slot]).start()
    for copy in dma:
        copy.start()
    done = 0
    for part in range(6):
        end = (part + 1) * (total // 6)
        while done < len(dma) and order[done][2] < end:
            dma[done].wait()
            done += 1

        def widen(t, _, base=part * (total // 6)):
            r0 = pl.multiple_of(base + t * 64, 64)
            for c in range(4):
                block = stage[pl.ds(r0, 64), c * 128 : (c + 1) * 128].astype(F32)
                table[pl.ds(r0 * 4 + c, 64, stride=4), :] = block
            return 0

        lax.fori_loop(0, total // 6 // 64, widen, 0)
    CH, BATCH = 128, 1024
    batches = idx_ref.shape[0] // BATCH

    def indices(batch, slot):
        part = pl.ds(pl.multiple_of(batch * BATCH, BATCH), BATCH)
        return pltpu.make_async_copy(idx_ref.at[part], rows_at.at[pl.ds(slot * BATCH, BATCH)], isem.at[slot])

    def chunk(p0, at):
        for lo in range(0, 2 * CH, 32):
            got = [table[pl.ds(pl.multiple_of(rows_at[at + lo + u], 4), 4), :] for u in range(32)]
            for u in range(32):
                picked[pl.ds((lo + u) * 4, 4), :] = got[u]
        for c in range(4):
            block = picked[pl.ds(c, CH, stride=4), :]
            left[c * 128 : (c + 1) * 128, pl.ds(p0, CH)] = block.T.astype(BF)
            block = picked[pl.ds(CH * 4 + c, CH, stride=4), :]
            right[pl.ds(p0, CH), c * 128 : (c + 1) * 128] = block.astype(BF)

    def two(t, _):
        for slot in range(2):
            batch = 2 * t + slot
            indices(batch, slot).wait()
            for k in range(BATCH // (2 * CH)):
                p0 = pl.multiple_of(batch * (BATCH // 2) + k * CH, CH)
                chunk(p0, slot * BATCH + k * 2 * CH)

            @pl.when(batch + 2 < batches)
            def _():
                indices(batch + 2, slot).start()

        return 0

    lax.fori_loop(0, batches // 2, two, 0)

    def multiply(t, _):
        jk, a0 = t // 2, pl.multiple_of((t % 2) * 256, 256)
        h = h_ref[pl.ds(jk, 1), :].astype(BF)
        scaled[...] = left[pl.ds(a0, 256), :] * h
        out_ref[jk, pl.ds(a0, 256), :] = jnp.dot(scaled[...], right[...], preferred_element_type=F32).astype(BF)
        return 0

    lax.fori_loop(0, 8, multiply, 0)


def last_stage(index, h, arrays, copies):
    pairs, total = index.shape[0] // 2, sum(c[3] for c in copies)
    return pl.pallas_call(
        functools.partial(last_kernel, copies, len(arrays)),
        out_shape=jax.ShapeDtypeStruct((4, 512, 512), BF),
        in_specs=[pl.BlockSpec(memory_space=pl.ANY), pl.BlockSpec(memory_space=pltpu.VMEM)]
        + [pl.BlockSpec(memory_space=pl.ANY)] * len(arrays),
        out_specs=pl.BlockSpec(memory_space=pltpu.VMEM),
        scratch_shapes=[
            pltpu.VMEM((total, 512), BF),
            pltpu.VMEM((total * 4, 128), F32),
            pltpu.VMEM((128 * 8, 128), F32),
            pltpu.VMEM((512, pairs), BF),
            pltpu.VMEM((pairs, 512), BF),
            pltpu.VMEM((256, pairs), BF),
            pltpu.SMEM((2048,), jnp.int32),
            pltpu.SemaphoreType.DMA((len(copies),)),
            pltpu.SemaphoreType.DMA((2,)),
        ],
        compiler_params=pltpu.CompilerParams(vmem_limit_bytes=60 * 1024 * 1024),
        cost_estimate=pl.CostEstimate(flops=9 * 10**9, bytes_accessed=15 * 10**6, transcendentals=0),
        name="gather_scale_dot",
    )(index, h, *arrays)


def stages(integrals, screen, occupied, virtual, pair_index):
    arrays, copies = gather_virtual(virtual)
    occ = gather_occupied(occupied)
    own = lax.dynamic_slice_in_dim(occ, lax.axis_index("orb") * 8, 8, 0)
    half = half_transform(integrals, block_place(screen), own, occ)
    sent = half.astype(BF).reshape(64, 4, half.shape[1])
    owned = lax.all_to_all(sent, "pair", 0, 0)
    h = owned.transpose(1, 0, 2).reshape(4, -1).astype(F32)
    index = virtual_place(pair_index).reshape(2, -1, 128).transpose(1, 0, 2).reshape(-1) * 4
    return last_stage(index, h, arrays, copies)[None]


def solution(mesh):
    placed = (
        P("pair", None, None, None),
        P(None, "pair", None),
        P(("pair", "orb"), None),
        P(("pair", "orb"), None),
        P(),
    )
    return jax.shard_map(stages, mesh=mesh, in_specs=placed, out_specs=P("orb", "pair", None, None), check_vma=False)
```

```python
import functools

import jax
import jax.numpy as jnp
from jax import lax
from jax.experimental import pallas as pl
from jax.experimental.pallas import tpu as pltpu
from jax.sharding import PartitionSpec as P

BLK = 128
NZ, NX, NY = 8, 4, 4
BF, F32 = jnp.bfloat16, jnp.float32


def pair_moves(dz=0, dx=0, dc=0):
    moves = []
    for z in range(NZ):
        for x in range(NX):
            for c in range(2):
                src = (((z + dz) % NZ) * NX + (x + dx) % NX) * 2 + (c + dc) % 2
                moves.append((src, (z * NX + x) * 2 + c))
    return moves


def fetch(value, axis, step):
    if axis == "y":
        return lax.ppermute(value, "orb", [((y + step) % NY, y) for y in range(NY)])
    return lax.ppermute(value, "pair", pair_moves(**{"d" + axis: step}))


def rows(*parts):
    return jnp.concatenate(parts, axis=0)


def four(value, axis):
    return [value] + [fetch(value, axis, step) for step in (1, 2, 3)]


def cross(value, step, swap):
    moves = []
    for z in range(NZ):
        for x in range(NX):
            for c in range(2):
                for y in range(NY):
                    ex, ey = (x, (y + step) % NY) if c == swap else ((x + step) % NX, y)
                    src = ((z * NX + ex) * 2 + c) * NY + ey
                    moves.append((src, ((z * NX + x) * 2 + c) * NY + y))
    return lax.ppermute(value, ("pair", "orb"), moves)


def ring(value, move):
    half = value.shape[0] // 2
    up, down = move(value, 1), move(value, -1)
    far = [move(up[:half], 1), move(down[half:], -1)]
    return [value, up, *far, down]


def gather_virtual(v):
    up, down = fetch(v, "z", 1), fetch(v, "z", -1)
    near = rows(down, v, up)
    far_up, far_down = fetch(near, "z", 3), fetch(near[48:], "z", -3)
    z_all = rows(near, far_up, far_down)
    b = rows(*ring(z_all, lambda t, d: cross(t, d, 0)))
    arrays = ring(b, lambda t, d: cross(t, d, 1))
    arrays = arrays + [fetch(t, "c", 1) for t in arrays]
    copies, at = [], 0
    for k, t in enumerate(arrays):
        copies.append((k, 0, at, t.shape[0]))
        at += t.shape[0]
    return arrays, copies


def place():
    pair, y = lax.axis_index("pair"), lax.axis_index("orb")
    return pair // 8, (pair // 2) % NX, pair % 2, y


def virtual_place(index):
    mz, mx, mc, my = place()
    device, local = index // 48, index % 48
    pair = device // NY
    dy = (device - my) % NY
    dc = (pair - mc) % 2
    dx = (pair // 2 - mx) % NX
    dz = (pair // 8 - mz) % NZ
    inner, outer = jnp.where(pair % 2 == 0, dy, dx), jnp.where(pair % 2 == 0, dx, dy)
    return dc * 6144 + outer * 1536 + inner * 384 + (dz + 1) % NZ * 48 + local


def gather_occupied(o):
    _, _, mc, my = place()
    ot = o.T
    row = jnp.zeros((32, 192), BF)
    pieces = four(ot, "y")
    for step, piece in enumerate(pieces):
        row = lax.dynamic_update_slice(row, piece, (0, ((my + step) % NY) * 48))
    other = fetch(row, "c", 1)
    chip = jnp.where(mc == 0, jnp.concatenate([row, other], 1), jnp.concatenate([other, row], 1))
    mine = lax.dynamic_slice_in_dim(chip, mc * 16, 16, 0)
    cols = lambda *t: jnp.concatenate(t, axis=1)
    near = cols(fetch(mine, "z", -1), mine, fetch(mine, "z", 1))
    far_up, far_down = fetch(near, "z", 3), fetch(near[:, 384:], "z", -3)
    z_all = cols(near, far_up, far_down)
    mine = cols(*four(z_all, "x"))
    other = fetch(mine, "c", 1)
    return jnp.where(mc == 0, rows(mine, other), rows(other, mine))


def block_place(block):
    mz, mx, _, _ = place()
    chip = block // 3
    dx = (chip - mx) % NX
    dz = (chip // NX - mz) % NZ
    return (dx * 8 + (dz + 1) % NZ) * 3 + block % 3


def half_kernel(group, scr_ref, own_ref, occ_ref, ints_ref, out_ref, ints, halves, sem):
    pairs = ints.shape[0]
    groups = pairs // group

    def copy(g):
        part = pl.ds(g * group, group)
        return pltpu.make_async_copy(ints_ref.at[part], ints.at[part], sem.at[g])

    for g in range(groups):
        copy(g).start()

    def step(g, _):
        copy(g).wait()
        firsts = []
        for t in range(group):
            p = g * group + t
            for s in range(8):
                m = pl.multiple_of(scr_ref[0, p, s] * BLK, BLK)
                first = jnp.dot(own_ref[:, pl.ds(m, BLK)], ints[p, s], preferred_element_type=F32)
                firsts.append(first.astype(BF))
        for t in range(group):
            p = g * group + t
            coefs = []
            for s in range(8):
                n = pl.multiple_of(scr_ref[1, p, s] * BLK, BLK)
                coefs.append(occ_ref[:, pl.ds(n, BLK)])
            value = lax.dot_general(
                jnp.concatenate(firsts[8 * t : 8 * t + 8], axis=1), jnp.concatenate(coefs, axis=1),
                (((1,), (1,)), ((), ())), preferred_element_type=F32,
            )
            halves[pl.ds(p, 8, stride=pairs), 0:32] = value
        return 0

    lax.fori_loop(0, groups, step, 0)
    for i in range(8):
        block = halves[i * pairs : (i + 1) * pairs, :].T
        out_ref[pl.ds(i, 32, stride=8), :] = block[0:32, :]


def half_transform(integrals, blocks, own, occ):
    pairs, group = integrals.shape[0], 8
    vmem = pl.BlockSpec(memory_space=pltpu.VMEM)
    return pl.pallas_call(
        functools.partial(half_kernel, group),
        in_specs=[pl.BlockSpec(memory_space=pltpu.SMEM), vmem, vmem, pl.BlockSpec(memory_space=pl.ANY)],
        out_specs=vmem,
        out_shape=jax.ShapeDtypeStruct((256, pairs), F32),
        scratch_shapes=[
            pltpu.VMEM(integrals.shape, BF),
            pltpu.VMEM((8 * pairs, 128), F32),
            pltpu.SemaphoreType.DMA((pairs // group,)),
        ],
        compiler_params=pltpu.CompilerParams(vmem_limit_bytes=48 * 1024 * 1024),
        cost_estimate=pl.CostEstimate(flops=3 * 10**8, bytes_accessed=18 * 10**6, transcendentals=0),
        name="half_transform",
    )(blocks, own, occ, integrals)


def last_kernel(copies, arrays, idx_ref, h_ref, *refs):
    pieces, out_ref = refs[:arrays], refs[arrays]
    stage, table, picked, left, right, scaled, rows_at, sem, isem = refs[arrays + 1 :]
    total = stage.shape[0]
    order = sorted(copies, key=lambda c: c[2])
    dma = [
        pltpu.make_async_copy(pieces[k].at[pl.ds(src, n)], stage.at[pl.ds(dst, n)], sem.at[j])
        for j, (k, src, dst, n) in enumerate(order)
    ]
    for slot in range(2):
        part = pl.ds(slot * 1024, 1024)
        pltpu.make_async_copy(idx_ref.at[part], rows_at.at[part], isem.at[slot]).start()
    for copy in dma:
        copy.start()
    done = 0
    for part in range(6):
        end = (part + 1) * (total // 6)
        while done < len(dma) and order[done][2] < end:
            dma[done].wait()
            done += 1

        def widen(t, _, base=part * (total // 6)):
            r0 = pl.multiple_of(base + t * 64, 64)
            for c in range(4):
                block = stage[pl.ds(r0, 64), c * 128 : (c + 1) * 128].astype(F32)
                table[pl.ds(r0 * 4 + c, 64, stride=4), :] = block
            return 0

        lax.fori_loop(0, total // 6 // 64, widen, 0)
    CH, BATCH = 128, 1024
    batches = idx_ref.shape[0] // BATCH

    def indices(batch, slot):
        part = pl.ds(pl.multiple_of(batch * BATCH, BATCH), BATCH)
        return pltpu.make_async_copy(idx_ref.at[part], rows_at.at[pl.ds(slot * BATCH, BATCH)], isem.at[slot])

    def chunk(p0, at):
        for lo in range(0, 2 * CH, 32):
            got = [table[pl.ds(pl.multiple_of(rows_at[at + lo + u], 4), 4), :] for u in range(32)]
            for u in range(32):
                picked[pl.ds((lo + u) * 4, 4), :] = got[u]
        for c in range(4):
            block = picked[pl.ds(c, CH, stride=4), :]
            left[c * 128 : (c + 1) * 128, pl.ds(p0, CH)] = block.T.astype(BF)
            block = picked[pl.ds(CH * 4 + c, CH, stride=4), :]
            right[pl.ds(p0, CH), c * 128 : (c + 1) * 128] = block.astype(BF)

    def two(t, _):
        for slot in range(2):
            batch = 2 * t + slot
            indices(batch, slot).wait()
            for k in range(BATCH // (2 * CH)):
                p0 = pl.multiple_of(batch * (BATCH // 2) + k * CH, CH)
                chunk(p0, slot * BATCH + k * 2 * CH)

            @pl.when(batch + 2 < batches)
            def _():
                indices(batch + 2, slot).start()

        return 0

    lax.fori_loop(0, batches // 2, two, 0)

    def multiply(t, _):
        jk, a0 = t // 2, pl.multiple_of((t % 2) * 256, 256)
        h = h_ref[pl.ds(jk, 1), :].astype(BF)
        scaled[...] = left[pl.ds(a0, 256), :] * h
        out_ref[jk, pl.ds(a0, 256), :] = jnp.dot(scaled[...], right[...], preferred_element_type=F32).astype(BF)
        return 0

    lax.fori_loop(0, 8, multiply, 0)


def last_stage(index, h, arrays, copies):
    pairs, total = index.shape[0] // 2, sum(c[3] for c in copies)
    return pl.pallas_call(
        functools.partial(last_kernel, copies, len(arrays)),
        out_shape=jax.ShapeDtypeStruct((4, 512, 512), BF),
        in_specs=[pl.BlockSpec(memory_space=pl.ANY), pl.BlockSpec(memory_space=pltpu.VMEM)]
        + [pl.BlockSpec(memory_space=pl.ANY)] * len(arrays),
        out_specs=pl.BlockSpec(memory_space=pltpu.VMEM),
        scratch_shapes=[
            pltpu.VMEM((total, 512), BF),
            pltpu.VMEM((total * 4, 128), F32),
            pltpu.VMEM((128 * 8, 128), F32),
            pltpu.VMEM((512, pairs), BF),
            pltpu.VMEM((pairs, 512), BF),
            pltpu.VMEM((256, pairs), BF),
            pltpu.SMEM((2048,), jnp.int32),
            pltpu.SemaphoreType.DMA((len(copies),)),
            pltpu.SemaphoreType.DMA((2,)),
        ],
        compiler_params=pltpu.CompilerParams(vmem_limit_bytes=60 * 1024 * 1024),
        cost_estimate=pl.CostEstimate(flops=9 * 10**9, bytes_accessed=15 * 10**6, transcendentals=0),
        name="gather_scale_dot",
    )(index, h, *arrays)


def stages(integrals, screen, occupied, virtual, pair_index):
    arrays, copies = gather_virtual(virtual)
    occ = gather_occupied(occupied)
    own = lax.dynamic_slice_in_dim(occ, lax.axis_index("orb") * 8, 8, 0)
    half = half_transform(integrals, block_place(screen), own, occ)
    sent = half.astype(BF).reshape(64, 4, half.shape[1])
    owned = lax.all_to_all(sent, "pair", 0, 0)
    h = owned.transpose(1, 0, 2).reshape(4, -1).astype(F32)
    index = virtual_place(pair_index).reshape(2, -1, 128).transpose(1, 0, 2).reshape(-1) * 4
    return last_stage(index, h, arrays, copies)[None]


def solution(mesh):
    placed = (
        P("pair", None, None, None),
        P(None, "pair", None),
        P(("pair", "orb"), None),
        P(("pair", "orb"), None),
        P(),
    )
    return jax.shard_map(stages, mesh=mesh, in_specs=placed, out_specs=P("orb", "pair", None, None), check_vma=False)
```

```python
import functools

import jax
import jax.numpy as jnp
from jax import lax
from jax.experimental import pallas as pl
from jax.experimental.pallas import tpu as pltpu
from jax.sharding import PartitionSpec as P

BLK = 128
NZ, NX, NY = 8, 4, 4
BF, F32 = jnp.bfloat16, jnp.float32


def pair_moves(dz=0, dx=0, dc=0):
    moves = []
    for z in range(NZ):
        for x in range(NX):
            for c in range(2):
                src = (((z + dz) % NZ) * NX + (x + dx) % NX) * 2 + (c + dc) % 2
                moves.append((src, (z * NX + x) * 2 + c))
    return moves


def fetch(value, axis, step):
    if axis == "y":
        return lax.ppermute(value, "orb", [((y + step) % NY, y) for y in range(NY)])
    return lax.ppermute(value, "pair", pair_moves(**{"d" + axis: step}))


def rows(*parts):
    return jnp.concatenate(parts, axis=0)


def four(value, axis):
    return [value] + [fetch(value, axis, step) for step in (1, 2, 3)]


def cross(value, step, swap):
    moves = []
    for z in range(NZ):
        for x in range(NX):
            for c in range(2):
                for y in range(NY):
                    ex, ey = (x, (y + step) % NY) if c == swap else ((x + step) % NX, y)
                    src = ((z * NX + ex) * 2 + c) * NY + ey
                    moves.append((src, ((z * NX + x) * 2 + c) * NY + y))
    return lax.ppermute(value, ("pair", "orb"), moves)


def ring(value, move):
    half = value.shape[0] // 2
    up, down = move(value, 1), move(value, -1)
    far = [move(up[:half], 1), move(down[half:], -1)]
    return [value, up, *far, down]


def gather_virtual(v):
    near = rows(fetch(v, "z", -1), v, fetch(v, "z", 1))
    far_up = fetch(near, "z", 3)
    far_down = fetch(near[48:], "z", -3)
    z_all = rows(near, far_up, far_down)
    b = rows(*ring(z_all, lambda t, d: cross(t, d, 0)))
    arrays = ring(b, lambda t, d: cross(t, d, 1))
    arrays = arrays + [fetch(t, "c", 1) for t in arrays]
    copies, at = [], 0
    for k, t in enumerate(arrays):
        copies.append((k, 0, at, t.shape[0]))
        at += t.shape[0]
    return arrays, copies


def place():
    pair, y = lax.axis_index("pair"), lax.axis_index("orb")
    return pair // 8, (pair // 2) % NX, pair % 2, y


def virtual_place(index):
    mz, mx, mc, my = place()
    device, local = index // 48, index % 48
    pair = device // NY
    dy = (device - my) % NY
    dc = (pair - mc) % 2
    dx = (pair // 2 - mx) % NX
    dz = (pair // 8 - mz) % NZ
    inner, outer = jnp.where(pair % 2 == 0, dy, dx), jnp.where(pair % 2 == 0, dx, dy)
    return dc * 6144 + outer * 1536 + inner * 384 + (dz + 1) % NZ * 48 + local


def gather_occupied(o):
    _, _, mc, my = place()
    ot = o.T
    row = jnp.zeros((32, 192), BF)
    for step, piece in enumerate(four(ot, "y")):
        row = lax.dynamic_update_slice(row, piece, (0, ((my + step) % NY) * 48))
    other = fetch(row, "c", 1)
    chip = jnp.where(mc == 0, jnp.concatenate([row, other], 1), jnp.concatenate([other, row], 1))
    mine = lax.dynamic_slice_in_dim(chip, mc * 16, 16, 0)
    cols = lambda *t: jnp.concatenate(t, axis=1)
    near = cols(fetch(mine, "z", -1), mine, fetch(mine, "z", 1))
    z_all = cols(near, fetch(near, "z", 3), fetch(near[:, 384:], "z", -3))
    mine = cols(*four(z_all, "x"))
    other = fetch(mine, "c", 1)
    return jnp.where(mc == 0, rows(mine, other), rows(other, mine))


def block_place(block):
    mz, mx, _, _ = place()
    chip = block // 3
    dx = (chip - mx) % NX
    dz = (chip // NX - mz) % NZ
    return (dx * 8 + (dz + 1) % NZ) * 3 + block % 3


def half_kernel(group, scr_ref, own_ref, occ_ref, ints_ref, out_ref, ints, halves, sem):
    pairs = ints.shape[0]
    groups = pairs // group

    def copy(g):
        part = pl.ds(g * group, group)
        return pltpu.make_async_copy(ints_ref.at[part], ints.at[part], sem.at[g])

    for g in range(groups):
        copy(g).start()

    def step(g, _):
        copy(g).wait()
        firsts = []
        for t in range(group):
            p = g * group + t
            for s in range(8):
                m = pl.multiple_of(scr_ref[0, p, s] * BLK, BLK)
                first = jnp.dot(own_ref[:, pl.ds(m, BLK)], ints[p, s], preferred_element_type=F32)
                firsts.append(first.astype(BF))
        for t in range(group):
            p = g * group + t
            coefs = []
            for s in range(8):
                n = pl.multiple_of(scr_ref[1, p, s] * BLK, BLK)
                coefs.append(occ_ref[:, pl.ds(n, BLK)])
            value = lax.dot_general(
                jnp.concatenate(firsts[8 * t : 8 * t + 8], axis=1), jnp.concatenate(coefs, axis=1),
                (((1,), (1,)), ((), ())), preferred_element_type=F32,
            )
            halves[pl.ds(p, 8, stride=pairs), 0:32] = value
        return 0

    lax.fori_loop(0, groups, step, 0)
    for i in range(8):
        block = halves[i * pairs : (i + 1) * pairs, :].T
        out_ref[pl.ds(i, 32, stride=8), :] = block[0:32, :]


def half_transform(integrals, blocks, own, occ):
    pairs, group = integrals.shape[0], 8
    vmem = pl.BlockSpec(memory_space=pltpu.VMEM)
    return pl.pallas_call(
        functools.partial(half_kernel, group),
        in_specs=[pl.BlockSpec(memory_space=pltpu.SMEM), vmem, vmem, pl.BlockSpec(memory_space=pl.ANY)],
        out_specs=vmem,
        out_shape=jax.ShapeDtypeStruct((256, pairs), F32),
        scratch_shapes=[
            pltpu.VMEM(integrals.shape, BF),
            pltpu.VMEM((8 * pairs, 128), F32),
            pltpu.SemaphoreType.DMA((pairs // group,)),
        ],
        compiler_params=pltpu.CompilerParams(vmem_limit_bytes=48 * 1024 * 1024),
        cost_estimate=pl.CostEstimate(flops=3 * 10**8, bytes_accessed=18 * 10**6, transcendentals=0),
        name="half_transform",
    )(blocks, own, occ, integrals)


def last_kernel(copies, arrays, idx_ref, h_ref, *refs):
    pieces, out_ref = refs[:arrays], refs[arrays]
    stage, table, picked, left, right, scaled, rows_at, sem, isem = refs[arrays + 1 :]
    total = stage.shape[0]
    order = sorted(copies, key=lambda c: c[2])
    dma = [
        pltpu.make_async_copy(pieces[k].at[pl.ds(src, n)], stage.at[pl.ds(dst, n)], sem.at[j])
        for j, (k, src, dst, n) in enumerate(order)
    ]
    for slot in range(2):
        part = pl.ds(slot * 1024, 1024)
        pltpu.make_async_copy(idx_ref.at[part], rows_at.at[part], isem.at[slot]).start()
    for copy in dma:
        copy.start()
    done = 0
    for part in range(6):
        end = (part + 1) * (total // 6)
        while done < len(dma) and order[done][2] < end:
            dma[done].wait()
            done += 1

        def widen(t, _, base=part * (total // 6)):
            r0 = pl.multiple_of(base + t * 64, 64)
            for c in range(4):
                block = stage[pl.ds(r0, 64), c * 128 : (c + 1) * 128].astype(F32)
                table[pl.ds(r0 * 4 + c, 64, stride=4), :] = block
            return 0

        lax.fori_loop(0, total // 6 // 64, widen, 0)
    CH, BATCH = 128, 1024
    batches = idx_ref.shape[0] // BATCH

    def indices(batch, slot):
        part = pl.ds(pl.multiple_of(batch * BATCH, BATCH), BATCH)
        return pltpu.make_async_copy(idx_ref.at[part], rows_at.at[pl.ds(slot * BATCH, BATCH)], isem.at[slot])

    def chunk(p0, at):
        for lo in range(0, 2 * CH, 32):
            got = [table[pl.ds(pl.multiple_of(rows_at[at + lo + u], 4), 4), :] for u in range(32)]
            for u in range(32):
                picked[pl.ds((lo + u) * 4, 4), :] = got[u]
        for c in range(4):
            block = picked[pl.ds(c, CH, stride=4), :]
            left[c * 128 : (c + 1) * 128, pl.ds(p0, CH)] = block.T.astype(BF)
            block = picked[pl.ds(CH * 4 + c, CH, stride=4), :]
            right[pl.ds(p0, CH), c * 128 : (c + 1) * 128] = block.astype(BF)

    def two(t, _):
        for slot in range(2):
            batch = 2 * t + slot
            indices(batch, slot).wait()
            for k in range(BATCH // (2 * CH)):
                p0 = pl.multiple_of(batch * (BATCH // 2) + k * CH, CH)
                chunk(p0, slot * BATCH + k * 2 * CH)

            @pl.when(batch + 2 < batches)
            def _():
                indices(batch + 2, slot).start()

        return 0

    lax.fori_loop(0, batches // 2, two, 0)

    def multiply(t, _):
        h = h_ref[pl.ds(t, 1), :].astype(BF)
        scaled[...] = left[...] * h
        out_ref[t] = jnp.dot(scaled[...], right[...], preferred_element_type=F32).astype(BF)
        return 0

    lax.fori_loop(0, 4, multiply, 0)


def last_stage(index, h, arrays, copies):
    pairs, total = index.shape[0] // 2, sum(c[3] for c in copies)
    return pl.pallas_call(
        functools.partial(last_kernel, copies, len(arrays)),
        out_shape=jax.ShapeDtypeStruct((4, 512, 512), BF),
        in_specs=[pl.BlockSpec(memory_space=pl.ANY), pl.BlockSpec(memory_space=pltpu.VMEM)]
        + [pl.BlockSpec(memory_space=pl.ANY)] * len(arrays),
        out_specs=pl.BlockSpec(memory_space=pltpu.VMEM),
        scratch_shapes=[
            pltpu.VMEM((total, 512), BF),
            pltpu.VMEM((total * 4, 128), F32),
            pltpu.VMEM((128 * 8, 128), F32),
            pltpu.VMEM((512, pairs), BF),
            pltpu.VMEM((pairs, 512), BF),
            pltpu.VMEM((512, pairs), BF),
            pltpu.SMEM((2048,), jnp.int32),
            pltpu.SemaphoreType.DMA((len(copies),)),
            pltpu.SemaphoreType.DMA((2,)),
        ],
        compiler_params=pltpu.CompilerParams(vmem_limit_bytes=60 * 1024 * 1024),
        cost_estimate=pl.CostEstimate(flops=9 * 10**9, bytes_accessed=15 * 10**6, transcendentals=0),
        name="gather_scale_dot",
    )(index, h, *arrays)


def stages(integrals, screen, occupied, virtual, pair_index):
    arrays, copies = gather_virtual(virtual)
    occ = gather_occupied(occupied)
    own = lax.dynamic_slice_in_dim(occ, lax.axis_index("orb") * 8, 8, 0)
    half = half_transform(integrals, block_place(screen), own, occ)
    sent = half.astype(BF).reshape(64, 4, half.shape[1])
    owned = lax.all_to_all(sent, "pair", 0, 0)
    h = owned.transpose(1, 0, 2).reshape(4, -1).astype(F32)
    index = virtual_place(pair_index).reshape(2, -1, 128).transpose(1, 0, 2).reshape(-1) * 4
    return last_stage(index, h, arrays, copies)[None]


def solution(mesh):
    placed = (
        P("pair", None, None, None),
        P(None, "pair", None),
        P(("pair", "orb"), None),
        P(("pair", "orb"), None),
        P(),
    )
    return jax.shard_map(stages, mesh=mesh, in_specs=placed, out_specs=P("orb", "pair", None, None), check_vma=False)
```
